32 devices in a mesh: cuts: 2 (over x), wide: 8 (over z, y), narrow: 2 (over core).
Axes of the slice: x: 2, y: 2, z: 4, core: 2. Of those that a mesh axis runs over, the one named last changes fastest.
Arguments:
- stem: float32 [2, 8192, 512], P(None, ('cuts', 'wide', 'narrow')), parts along dimension 1, may hold values from -6 to 6
- branches: float32 [3, 2, 512, 512], replicated, may hold values from -0.1875 to 0.1875
- perm: int32 [3, 512], replicated, may hold values from 0 to 511, each once within a row
- phase_table: float32 [3, 512], replicated, may hold values from -3.140625 to 3.140625
- slice_pick: int32 [6], P('cuts'), parts along dimension 0, may hold values from 0 to 2, each once
- half_net: float32 [2, 4096, 512], P(None, 'wide'), may hold values from -0.1875 to 0.1875
Outputs:
- amps: float32 [2, 4096, 4096], P(None, ('cuts', 'wide'), 'narrow'), parts along dimension 1
The draws below stay inside these ranges and needn't reach their ends.
There are 2 independent parts, one for each index of `cuts`. The reference program is written for one: setup_inputs(seed, part) draws one part's arguments, and reference() takes and returns one part's arrays. A program takes and returns all parts, laid end to end along the dimension named above; an argument that names none is the same for every part. Nothing has to cross between parts.
Inputs may be any that keep to these rules, and one draw needn't show every extreme that they name: `perm`: each row is a permutation of 0 .. 511. `slice_pick`: a permutation of 0 .. 2.
All inputs are finite; a program needn't handle non-finite values.
Results may differ from the reference program's by a relative error of at most 0.0001.
Values sent between devices are 32-bit elements; how exact they have to be, the bound alone decides.
No kernel may reach another device: no remote copies, remote signals or barrier semaphores. Data moves between devices by JAX's collectives and lax.ppermute only.
A program may use at most 128 MiB of HBM per device.

```python
import jax
import jax.numpy as jnp
from jax import lax

K = 512
HW = 4096
ROWS_DEV = 256
ROUNDS = 3
RW = 2048
R = 4096
N_WIDE = 8
N_NARROW = 2


def block_scale(key, shape, cuts, least, high):
    gain, own = 1.0, jax.random.fold_in(key, 6)
    for axis_at, shards_of in cuts:
        draws = jnp.exp(jax.random.uniform(jax.random.fold_in(own, axis_at), (shards_of,), jnp.float32, least / len(cuts), high / len(cuts)))
        gain = gain * jnp.repeat(draws, shape[axis_at] // shards_of).reshape([-1 if axis == axis_at else 1 for axis in range(len(shape))])
    return gain


def centred(key, shape, deviation, bound, shards=(), held_as=jnp.bfloat16):
    loudness = block_scale(key, shape, shards, -0.22, 0.18) if shards else 1.0
    drawn = jax.random.normal(key, shape, jnp.float32) * deviation * loudness
    return jnp.minimum(jnp.maximum(drawn, -bound), bound).astype(held_as)


def setup_inputs(seed: int = 0, part: int = 0) -> dict:
    streams_of = jax.random.split(jax.random.key(seed), 7)
    part_splits = jax.random.split(jax.random.fold_in(streams_of[6], part), 7)
    stem = centred(part_splits[0], (2, R, K), 1.0, 6.0, ((1, 16),), jnp.float32)
    branches = centred(streams_of[1], (ROUNDS, 2, K, K), (2 * K) ** -0.5, 0.1875, (), jnp.float32)
    perm = jax.vmap(lambda own: jax.random.permutation(own, K))(jax.random.split(streams_of[2], ROUNDS)).reshape((ROUNDS, K)).astype(jnp.int32)
    phase_table = jnp.clip(jax.random.uniform(streams_of[3], (ROUNDS, K), jnp.float32, -3.140625, 3.140625), -3.140625, 3.140625)
    slice_pick = jax.random.permutation(part_splits[4], ROUNDS).astype(jnp.int32)
    half_net = centred(streams_of[5], (2, HW, K), (2 * K) ** -0.5, 0.1875, ((1, 8),), jnp.float32)
    return dict(stem=stem, branches=branches, perm=perm, phase_table=phase_table, slice_pick=slice_pick, half_net=half_net)


def complex_dot(left, right):
    hp = lax.Precision.HIGHEST
    real = jnp.dot(left[0], right[0], precision=hp, preferred_element_type=jnp.float32) - jnp.dot(left[1], right[1], precision=hp, preferred_element_type=jnp.float32)
    imag = jnp.dot(left[0], right[1], precision=hp, preferred_element_type=jnp.float32) + jnp.dot(left[1], right[0], precision=hp, preferred_element_type=jnp.float32)
    return jnp.stack([real, imag])


def complex_cross(left, right):
    hp = lax.Precision.HIGHEST
    real = jnp.einsum("mk,nk->mn", left[0], right[0], precision=hp, preferred_element_type=jnp.float32) - jnp.einsum("mk,nk->mn", left[1], right[1], precision=hp, preferred_element_type=jnp.float32)
    imag = jnp.einsum("mk,nk->mn", left[0], right[1], precision=hp, preferred_element_type=jnp.float32) + jnp.einsum("mk,nk->mn", left[1], right[0], precision=hp, preferred_element_type=jnp.float32)
    return jnp.stack([real, imag])


def apply_round(block, phase, matrix):
    cosine = jnp.cos(phase)
    sine = jnp.sin(phase)
    rotated = jnp.stack([block[0] * cosine - block[1] * sine, block[0] * sine + block[1] * cosine])
    return complex_dot(rotated, matrix)


def reference(stem, branches, perm, phase_table, slice_pick, half_net):
    state = stem
    for turn in range(ROUNDS):
        if turn % 2 == 0:
            viewed = state.reshape(2, N_WIDE, N_NARROW, ROWS_DEV, N_WIDE, K // N_WIDE)
            state = jnp.transpose(viewed, (0, 4, 2, 3, 1, 5)).reshape(2, R, K)
        else:
            viewed = state.reshape(2, N_WIDE, N_NARROW, ROWS_DEV, N_NARROW, K // N_NARROW)
            state = jnp.transpose(viewed, (0, 1, 4, 3, 2, 5)).reshape(2, R, K)
        phase = lax.dynamic_index_in_dim(phase_table, slice_pick[turn], 0, keepdims=False)
        matrix = jnp.take(branches[turn], perm[turn], axis=1)
        state = apply_round(state, phase, matrix)
    joined = complex_cross(state, half_net)
    return joined.reshape(2, N_WIDE, N_NARROW, ROWS_DEV, HW).sum(axis=2).reshape(2, RW, HW)
```

```python
import jax
import jax.numpy as jnp
from jax import lax
from jax.sharding import PartitionSpec as P

AXES = ("cuts", "wide", "narrow")
HI = lax.Precision.HIGH


def mm(left, right):
    return jnp.dot(left, right, precision=HI, preferred_element_type=jnp.float32)


def mm_t(left, right):
    return lax.dot_general(
        left, right, (((1,), (1,)), ((), ())), precision=HI, preferred_element_type=jnp.float32
    )


def make_body(cuts, wide, narrow):
    tall = wide // 2
    part = tall // narrow

    def device(c, z, y, n):
        return (c * wide + z * 2 + y) * narrow + n

    def all_places():
        return [
            (c, z, y, n)
            for c in range(cuts)
            for z in range(tall)
            for y in range(2)
            for n in range(narrow)
        ]

    def holds(z, n, step):
        return ((z - step) % tall) // part == n

    def send(value, move, steps=None):
        pairs = []
        for place in all_places():
            to = move(*place)
            if steps is None or any(holds(to[1], to[3], s) for s in steps):
                pairs.append((device(*place), device(*to)))
        return lax.ppermute(value, AXES, pairs)

    def to_y(c, z, y, n):
        return (c, z, 1 - y, n)

    def to_x(c, z, y, n):
        return (c ^ 1, z, y, n)

    def gather_half(half_net, c):
        own = lax.dynamic_index_in_dim(half_net, c % 2, 0, keepdims=False)
        other = lax.dynamic_index_in_dim(half_net, 1 - c % 2, 0, keepdims=False)
        right = {0: own}
        left = {0: own}
        for s in range(1, tall // 2 + 1):
            right[s] = send(right[s - 1], lambda c, z, y, n: (c, (z + 1) % tall, y, n), (s,))
            if s < tall - tall // 2:
                left[s] = send(
                    left[s - 1], lambda c, z, y, n: (c, (z - 1) % tall, y, n), (tall - s,)
                )
        own_y = send(own, to_y, (0,))
        own_yx = send(own_y, to_x, (0,))
        slots = []
        for e in range(1, part):
            near = right[e] + left[part - e]
            near_y = send(near, to_y)
            near_x = send(near, to_x)
            near_d = send(near_y, to_x)
            slots.append((near, near_x, near_y, near_d))
        far = right[part]
        far_y = send(far, to_y, (part,))
        far_x = send(far, to_x, (part,))
        far_d = send(far_x, to_y, (part,))
        z = lax.axis_index("wide") // 2
        mine = z // part == lax.axis_index("narrow")
        first = (
            jnp.where(mine, own, far),
            jnp.where(mine, other, far_x),
            jnp.where(mine, own_y, far_y),
            jnp.where(mine, own_yx, far_d),
        )
        return [first] + slots

    def matrix(branches, perm, phase_table, slice_pick, turn):
        phase = lax.dynamic_index_in_dim(phase_table, slice_pick[turn], 0, keepdims=False)
        cosine = jnp.cos(phase)[:, None]
        sine = jnp.sin(phase)[:, None]
        m = jnp.take(branches[turn], perm[turn], axis=1)
        return jnp.stack([m[0] * cosine - m[1] * sine, m[0] * sine + m[1] * cosine])

    def body(stem, branches, perm, phase_table, slice_pick, half_net):
        rows = stem.shape[1]
        k = stem.shape[2]
        block = k // wide
        c = lax.axis_index("cuts")
        w = lax.axis_index("wide")
        n = lax.axis_index("narrow")
        packed = stem.reshape(2, rows, wide, block).transpose(2, 1, 0, 3).reshape(wide, rows, 2 * block)
        moved = lax.all_to_all(packed, "wide", split_axis=0, concat_axis=0, tiled=True)
        moved = moved.transpose(1, 0, 2).reshape(rows, 2 * k)
        slots = gather_half(half_net, c)
        m0 = matrix(branches, perm, phase_table, slice_pick, 0)
        m1 = matrix(branches, perm, phase_table, slice_pick, 1)
        m2 = matrix(branches, perm, phase_table, slice_pick, 2)
        fold = k // narrow
        m0 = m0.reshape(2, k, narrow, fold).sum(axis=2)
        b0 = jnp.stack([jnp.concatenate([m0[0], m0[1]], 1), jnp.concatenate([-m0[1], m0[0]], 1)])
        b0 = b0.reshape(2, wide, block, 2 * fold).transpose(1, 0, 2, 3).reshape(2 * k, 2 * fold)
        folded = mm(moved, b0)
        sub = rows // narrow
        mine = lax.dynamic_slice_in_dim(folded, n * sub, sub, 0)
        theirs = lax.dynamic_slice_in_dim(folded, (1 - n) * sub, sub, 0)
        got = lax.ppermute(theirs, "narrow", [(0, 1), (1, 0)])
        b1 = jnp.stack([m1[0].reshape(k, wide, block), m1[1].reshape(k, wide, block)], 2)
        b1i = jnp.stack([-m1[1].reshape(k, wide, block), m1[0].reshape(k, wide, block)], 2)
        b1 = b1.reshape(narrow, fold, 2 * k)
        b1i = b1i.reshape(narrow, fold, 2 * k)
        b1 = jnp.stack([b1, b1i], 1).reshape(narrow, 2 * fold, 2 * k)
        b1_mine = lax.dynamic_index_in_dim(b1, n, 0, keepdims=False)
        b1_theirs = lax.dynamic_index_in_dim(b1, 1 - n, 0, keepdims=False)
        summed = mm(mine, b1_mine) + mm(got, b1_theirs)
        packed = summed.reshape(sub, wide, 2 * block).transpose(1, 0, 2)
        moved = lax.all_to_all(packed, "wide", split_axis=0, concat_axis=0, tiled=True)
        moved = moved.transpose(1, 0, 2).reshape(sub, 2 * k)
        b2 = jnp.stack([jnp.concatenate([m2[0], m2[1]], 1), jnp.concatenate([-m2[1], m2[0]], 1)])
        b2 = b2.reshape(2, wide, block, 2 * k).transpose(1, 0, 2, 3).reshape(2 * k, 2 * k)
        state = mm(moved, b2)
        got = lax.ppermute(state, "narrow", [(0, 1), (1, 0)])
        first = jnp.where(n == 0, state, got)
        second = jnp.where(n == 0, got, state)
        state = jnp.concatenate([first, second], 0)
        real, imag = state[:, :k], state[:, k:]
        a_real = jnp.concatenate([real, imag], 0)
        a_imag = jnp.concatenate([-imag, real], 0)
        even = c % 2 == 0
        a_c = jnp.where(even, a_real, a_imag)
        a_o = jnp.where(even, a_imag, a_real)
        z = w // 2
        y = w % 2
        h = half_net.shape[1]
        out = jnp.zeros((2, rows, part * 2 * h), jnp.float32)
        for e, (yc, yo, oc, oo) in enumerate(slots):
            base = ((z - e) % part) * 2
            own_y = (mm_t(a_c, yc) + mm_t(a_o, yo)).reshape(2, rows, h)
            other_y = (mm_t(a_c, oc) + mm_t(a_o, oo)).reshape(2, rows, h)
            out = lax.dynamic_update_slice(out, own_y, (0, 0, (base + y) * h))
            out = lax.dynamic_update_slice(out, other_y, (0, 0, (base + 1 - y) * h))
        return out

    return body


def solution(mesh):
    placed = (
        P(None, AXES, None),
        P(),
        P(),
        P(),
        P("cuts"),
        P(None, "wide", None),
    )
    return jax.shard_map(
        make_body(*(mesh.shape[a] for a in AXES)),
        mesh=mesh,
        in_specs=placed,
        out_specs=P(None, ("cuts", "wide"), "narrow"),
        check_vma=False,
    )
```

```python
import functools

import jax
import jax.numpy as jnp
from jax import lax
from jax.experimental import pallas as pl
from jax.experimental.pallas import tpu as pltpu
from jax.sharding import PartitionSpec as P

AXES = ("cuts", "wide", "narrow")
F32 = jnp.float32
BF16 = jnp.bfloat16
WHOLE = pl.BlockSpec(memory_space=pltpu.VMEM)
SCALARS = pl.BlockSpec(memory_space=pltpu.SMEM)


def split(x):
    high = x.astype(BF16)
    return high, (x - high.astype(F32)).astype(BF16)


def dot3(left, right, dims=((1,), (0,))):
    one = lambda a, b: lax.dot_general(a, b, (dims, ((), ())), preferred_element_type=F32)
    return one(left[0], right[0]) + (one(left[0], right[1]) + one(left[1], right[0]))


def put(pair_refs, at, value):
    high, low = split(value)
    pair_refs[0][at] = high
    pair_refs[1][at] = low


def interleave(real, imag, block, index):
    return jnp.concatenate(
        [real[:, index * block : (index + 1) * block], imag[:, index * block : (index + 1) * block]], 1
    )


def start_kernel(part_ref, stem_ref, half_ref, packed_ref, own_ref, *, wide, narrow):
    block = stem_ref.shape[2] // wide
    sub = stem_ref.shape[1] // narrow
    for a in range(wide):
        both = interleave(stem_ref[0], stem_ref[1], block, a)
        for n in range(narrow):
            packed_ref[a * narrow + n] = both[n * sub : (n + 1) * sub]
    own_ref[...] = half_ref[0]


def prep_kernel(pick_ref, branches_ref, perm_ref, trig_ref, b0h, b0l, b1h, b1l, b2h, b2l, *, wide, narrow):
    k = branches_ref.shape[2]
    block = k // wide
    fold = k // narrow
    rounds = branches_ref.shape[0]
    rows = [perm_ref[t : t + 1, :].astype(F32) for t in range(rounds)]
    for t in range(rounds):
        rows += [trig_ref[0, pl.ds(pick_ref[t], 1), :], trig_ref[1, pl.ds(pick_ref[t], 1), :]]
    rows.append(jnp.zeros((16 - len(rows), k), F32))
    columns = jnp.concatenate(rows, 0).T
    lane = lax.broadcasted_iota(jnp.int32, (k, k), 1)
    for t in range(rounds):
        chosen = (lane == columns[:, t : t + 1].astype(jnp.int32)).astype(BF16)
        cosine = columns[:, rounds + 2 * t : rounds + 2 * t + 1]
        sine = columns[:, rounds + 2 * t + 1 : rounds + 2 * t + 2]

        def gathered(p):
            high, low = split(branches_ref[t, p])
            return jnp.dot(chosen, high, preferred_element_type=F32) + jnp.dot(
                chosen, low, preferred_element_type=F32
            )

        mr, mi = gathered(0), gathered(1)
        real, imag = mr * cosine - mi * sine, mr * sine + mi * cosine
        if t == 0:
            real = sum(real[:, i * fold : (i + 1) * fold] for i in range(narrow))
            imag = sum(imag[:, i * fold : (i + 1) * fold] for i in range(narrow))
        size = real.shape[1]
        refs = ((b0h, b0l), (b1h, b1l), (b2h, b2l))[t]
        chunk = fold if t == 1 else block
        for p, (one, two) in enumerate(((real, imag), (-imag, real))):
            oneh, onel = split(one)
            twoh, twol = split(two)
            for w in range(k // chunk):
                to = pl.ds((w * 2 + p) * chunk, chunk)
                src = slice(w * chunk, (w + 1) * chunk)
                refs[0][to, :size] = oneh[src]
                refs[0][to, size:] = twoh[src]
                refs[1][to, :size] = onel[src]
                refs[1][to, size:] = twol[src]


def rounds_kernel(moved_ref, b0h, b0l, b1h, b1l, out_ref, left_h, left_l, next_h, next_l, *, wide, narrow):
    sub, width = moved_ref.shape[1:]
    for i in range(wide):
        for n in range(narrow):
            high, low = split(moved_ref[i * narrow + n])
            left_h[n * sub : (n + 1) * sub, i * width : (i + 1) * width] = high
            left_l[n * sub : (n + 1) * sub, i * width : (i + 1) * width] = low
    folded = dot3((left_h[...], left_l[...]), (b0h[...], b0l[...]))
    high, low = split(folded)
    size = folded.shape[1]
    for n in range(narrow):
        next_h[:, n * size : (n + 1) * size] = high[n * sub : (n + 1) * sub]
        next_l[:, n * size : (n + 1) * size] = low[n * sub : (n + 1) * sub]
    summed = dot3((next_h[...], next_l[...]), (b1h[...], b1l[...]))
    k = summed.shape[1] // 2
    for a in range(wide):
        out_ref[a] = interleave(summed[:, :k], summed[:, k:], k // wide, a)


def last_kernel(moved_ref, b2h, b2l, out_ref, left_h, left_l, *, wide):
    width = moved_ref.shape[2]
    for i in range(wide):
        high, low = split(moved_ref[i])
        left_h[:, i * width : (i + 1) * width] = high
        left_l[:, i * width : (i + 1) * width] = low
    out_ref[...] = dot3((left_h[...], left_l[...]), (b2h[...], b2l[...]))


def left_kernel(info_ref, mine_ref, got_ref, high_ref, low_ref):
    n, c = info_ref[0], info_ref[1]
    sub = mine_ref.shape[0]
    k = mine_ref.shape[1] // 2

    def side(from_ref, core):
        real, imag = from_ref[:, :k], from_ref[:, k:]
        for at, by_real, by_imag in ((0, real, -imag), (1, imag, real)):
            to = pl.ds((at * 2 + core) * sub, sub)
            for column, value in (
                (0, jnp.where(c == 0, by_real, by_imag)),
                (1, jnp.where(c == 0, by_imag, by_real)),
            ):
                high, low = split(value)
                high_ref[to, column * k : (column + 1) * k] = high
                low_ref[to, column * k : (column + 1) * k] = low

    side(mine_ref, n)
    side(got_ref, 1 - n)


def join_kernel(info_ref, lh, ll, *refs, pieces):
    k = lh.shape[1] // 2
    ins, out_ref = refs[:-2], refs[-1]
    total = None
    at = 0
    for column, count in enumerate(pieces):
        value = ins[at][...].reshape(ins[at].shape[-2:])
        if count == 2:
            value = jnp.where(info_ref[1] == 1, value, ins[at + 1][...])
        at += count
        cols = slice(column * k, (column + 1) * k)
        term = dot3((lh[:, cols], ll[:, cols]), split(value), ((1,), (1,)))
        total = term if total is None else total + term
    out_ref[...] = total.reshape(out_ref.shape)


def call(kernel, out, ins, scratch=(), **params):
    return pl.pallas_call(
        functools.partial(kernel, **params),
        out_shape=[jax.ShapeDtypeStruct(s, d) for s, d in out],
        in_specs=[SCALARS if jnp.issubdtype(x.dtype, jnp.integer) and x.ndim == 1 else WHOLE for x in ins],
        out_specs=[WHOLE] * len(out),
        scratch_shapes=[pltpu.VMEM(s, d) for s, d in scratch],
    )(*ins)


def make_body(cuts, wide, narrow):
    tall = wide // 2
    part = tall // narrow

    def device(c, z, y, n):
        return (c * wide + z * 2 + y) * narrow + n

    places = [
        (c, z, y, n)
        for c in range(cuts)
        for z in range(tall)
        for y in range(2)
        for n in range(narrow)
    ]

    def send(value, move, step=None):
        pairs = []
        for place in places:
            to = move(*place)
            if step is None or ((to[1] - step) % tall) // part == to[3]:
                pairs.append((device(*place), device(*to)))
        return lax.ppermute(value, AXES, pairs)

    def up(c, z, y, n):
        return (c, (z + 1) % tall, y, n)

    def down(c, z, y, n):
        return (c, (z - 1) % tall, y, n)

    def to_y(c, z, y, n):
        return (c, z, 1 - y, n)

    def to_x(c, z, y, n):
        return (c ^ 1, z, y, n)

    def swap_cores(c, z, y, n):
        return (c, z, y, 1 - n)

    def body(stem, branches, perm, phase_table, slice_pick, half_net):
        rows, k = stem.shape[1:]
        h = half_net.shape[1]
        sub = rows // narrow
        block = k // wide
        fold = k // narrow
        c = lax.axis_index("cuts") % 2
        w = lax.axis_index("wide")
        n = lax.axis_index("narrow")
        z, y = w // 2, w % 2
        sizes = dict(wide=wide, narrow=narrow)

        packed, own = pl.pallas_call(
            functools.partial(start_kernel, **sizes),
            out_shape=[
                jax.ShapeDtypeStruct((wide * narrow, sub, 2 * block), F32),
                jax.ShapeDtypeStruct((h, k), F32),
            ],
            grid_spec=pltpu.PrefetchScalarGridSpec(
                num_scalar_prefetch=1,
                grid=(1,),
                in_specs=[
                    pl.BlockSpec((2, rows, k), lambda i, p: (0, 0, 0)),
                    pl.BlockSpec((1, h, k), lambda i, p: (p[0], 0, 0)),
                ],
                out_specs=[
                    pl.BlockSpec((wide * narrow, sub, 2 * block), lambda i, p: (0, 0, 0)),
                    pl.BlockSpec((h, k), lambda i, p: (0, 0)),
                ],
            ),
        )(c.reshape(1), stem, half_net)
        moved = lax.all_to_all(packed, ("wide", "narrow"), split_axis=0, concat_axis=0, tiled=True)

        right, left = {0: own}, {0: own}
        for s in range(1, part * narrow // 2 + 1):
            right[s] = send(right[s - 1], up, s)
            if s < tall - tall // 2:
                left[s] = send(left[s - 1], down, tall - s)
        own_y = send(own, to_y, 0)
        own_yx = send(own_y, to_x, 0)
        slots = []
        for e in range(1, part):
            near = right[e] + left[part - e]
            near_y = send(near, to_y)
            near_x = send(near, to_x)
            slots.append((near, near_x, near_y, send(near_y, to_x)))
        far = right[part]
        far_y = send(far, to_y, part)
        far_x = send(far, to_x, part)
        far_d = send(far_x, to_y, part)

        trig = jnp.stack([jnp.cos(phase_table), jnp.sin(phase_table)])
        b0h, b0l, b1h, b1l, b2h, b2l = call(
            prep_kernel,
            [((2 * k, 2 * fold), BF16)] * 2 + [((2 * k, 2 * k), BF16)] * 4,
            (slice_pick, branches, perm, trig),
            **sizes,
        )
        (summed,) = call(
            rounds_kernel,
            [((wide, sub, 2 * block), F32)],
            (moved, b0h, b0l, b1h, b1l),
            [((rows, 2 * k), BF16)] * 2 + [((sub, 2 * k), BF16)] * 2,
            **sizes,
        )
        moved = lax.all_to_all(summed, "wide", split_axis=0, concat_axis=0, tiled=True)
        (state,) = call(
            last_kernel,
            [((sub, 2 * k), F32)],
            (moved, b2h, b2l),
            [((sub, 2 * k), BF16)] * 2,
            wide=wide,
        )
        got = send(state, swap_cores)
        lh, ll = call(
            left_kernel, [((2 * rows, 2 * k), BF16)] * 2, (jnp.stack([n, c]), state, got)
        )

        mine = (z // part == n).astype(jnp.int32)

        def join(out, column, first, second):
            info = jnp.stack([column, mine, c, 1 - c])
            ins, specs, pieces = [], [], []
            for where, values in ((2, first), (3, second)):
                pieces.append(len(values))
                for value in values:
                    ins.append(value)
                    if value.ndim == 3:
                        specs.append(pl.BlockSpec((1, h, k), lambda i, s, where=where: (s[where], 0, 0)))
                    else:
                        specs.append(pl.BlockSpec((h, k), lambda i, s: (0, 0)))
            left_spec = pl.BlockSpec((2 * rows, 2 * k), lambda i, s: (0, 0))
            aliases = {}
            shape = (2, rows, part * 2 * h)
            if out is not None:
                aliases = {3 + len(ins): 0}
            ins.append(jnp.zeros((8, 128), F32) if out is None else out)
            specs.append(pl.BlockSpec(memory_space=pl.ANY))
            return pl.pallas_call(
                functools.partial(join_kernel, pieces=tuple(pieces)),
                out_shape=jax.ShapeDtypeStruct(shape, F32),
                grid_spec=pltpu.PrefetchScalarGridSpec(
                    num_scalar_prefetch=1,
                    grid=(1,),
                    in_specs=[left_spec, left_spec] + specs,
                    out_specs=pl.BlockSpec((2, rows, h), lambda i, s: (0, 0, s[0])),
                ),
                input_output_aliases=aliases,
            )(info, lh, ll, *ins)

        out = None
        for e, (near, near_x, near_y, near_d) in enumerate(slots, 1):
            base = ((z - e) % part) * 2
            out = join(out, base + y, (near,), (near_x,))
            out = join(out, base + 1 - y, (near_y,), (near_d,))
        base = (z % part) * 2
        out = join(out, base + y, (half_net, far), (half_net, far_x))
        out = join(out, base + 1 - y, (own_y, far_y), (own_yx, far_d))
        return out

    return body


def solution(mesh):
    placed = (
        P(None, AXES, None),
        P(),
        P(),
        P(),
        P("cuts"),
        P(None, "wide", None),
    )
    return jax.shard_map(
        make_body(*(mesh.shape[a] for a in AXES)),
        mesh=mesh,
        in_specs=placed,
        out_specs=P(None, ("cuts", "wide"), "narrow"),
        check_vma=False,
    )
```
